32 devices in a mesh: sweep: 8 (over z, y), tile: 4 (over x, core).
Axes of the slice: x: 2, y: 2, z: 4, core: 2. Of those that a mesh axis runs over, the one named last changes fastest.
Arguments:
- sources: float32 [8, 8, 4096], P('sweep', None, 'tile'), may hold values from -6 to 6
- blocks: bfloat16 [8, 32, 4, 64, 128], P('sweep', 'tile'), may hold values from -1.1 to 1.1
- pattern: int32 [8, 32, 3], P('sweep', 'tile'), may hold values from 0 to 31, as said below
Outputs:
- upper: float32 [8, 8, 4096], P('sweep', None, 'tile')
The draws below stay inside these ranges and needn't reach their ends.
Inputs may be any that keep to these rules, and one draw needn't show every extreme that they name: `pattern`: the column blocks of one block row are distinct and differ from the row block.
All inputs are finite; a program needn't handle non-finite values.
Results may differ from the reference program's by a relative error of at most 0.0048.
Values may be sent and summed in bfloat16 or wider, within the bound.
No kernel may reach another device: no remote copies, remote signals or barrier semaphores. Data moves between devices by JAX's collectives and lax.ppermute only.
A program may use at most 64 MiB of HBM per device.

```python
import math
import jax
import jax.numpy as jnp
from jax import lax

BLOCK = 64
RHS = 8
K_OFF = 3
SEG = 4
LAY_DEV = 1
NBLK = 32
LAYERS = 8


def draw_blocks(key, part):
    key_noise = jax.random.fold_in(key, 11)
    key_rho = jax.random.fold_in(key, 12)
    key_angle = jax.random.fold_in(key, 13)
    sigma = 0.35 / math.sqrt(2.0 * BLOCK * (K_OFF + 1))
    noise = jax.random.normal(key_noise, (LAYERS, NBLK, K_OFF + 1, BLOCK, 2 * BLOCK), jnp.float32)
    noise = jnp.clip(noise, -4.0, 4.0) * sigma
    log_rho = jax.random.uniform(key_rho, (LAYERS, NBLK, BLOCK), jnp.float32, math.log(0.5), math.log(0.93))
    radius = jnp.exp(log_rho)
    angle = jax.random.uniform(key_angle, (LAYERS, NBLK, BLOCK), jnp.float32, -math.pi, math.pi)
    out_idx = jnp.arange(BLOCK, dtype=jnp.int32)[:, None]
    in_idx = jnp.arange(2 * BLOCK, dtype=jnp.int32)[None, :]
    real_eye = (in_idx == out_idx).astype(jnp.float32)
    imag_eye = (in_idx == out_idx + BLOCK).astype(jnp.float32)
    diagonal = (radius * jnp.cos(angle))[..., None] * real_eye + (radius * jnp.sin(angle))[..., None] * imag_eye
    first = noise[:, :, 0] + diagonal
    full = jnp.concatenate([first[:, :, None], noise[:, :, 1:]], axis=2)
    return full.astype(jnp.bfloat16)


def draw_pattern(key, part):
    scores = jax.random.randint(key, (LAYERS, NBLK, NBLK - 1), 0, 1 << 20) * (NBLK - 1)
    scores = scores + jnp.arange(NBLK - 1, dtype=jnp.int32)
    order = jnp.argsort(scores, axis=-1, stable=True)[..., :K_OFF].astype(jnp.int32)
    row_ids = jnp.arange(NBLK, dtype=jnp.int32)[None, :, None]
    return ((row_ids + order + 1) % NBLK).astype(jnp.int32)


def block_scale(rng, extent, shards, least, high):
    def one(dim, shards_of):
        draws = jax.random.uniform(jax.random.fold_in(jax.random.fold_in(rng, 6), dim), (shards_of,), jnp.float32, least / len(shards), high / len(shards))
        return jnp.repeat(jnp.exp(draws), extent[dim] // shards_of).reshape((-1,) + (1,) * (len(extent) - dim - 1))

    factor_of = one(*shards[0])
    for cut in shards[1:]:
        factor_of = factor_of * one(*cut)
    return factor_of


def scatter_about(key, shape, scale, reach, split=(), kind=jnp.bfloat16):
    gain = block_scale(key, shape, split, -0.22, 0.18) if split else 1.0
    values = jax.random.normal(key, shape, jnp.float32) * scale * gain
    return jnp.minimum(jnp.maximum(values, -reach), reach).astype(kind)


def setup_inputs(seed: int = 0) -> dict:
    seeds = jax.random.split(jax.random.key(seed), 4)
    sources = scatter_about(seeds[0], (LAYERS, RHS, NBLK * 2 * BLOCK), 1.0, 6.0, ((0, 8), (2, 4)), jnp.float32)
    blocks = draw_blocks(jax.random.fold_in(seeds[3], 71), 0)
    pattern = draw_pattern(jax.random.fold_in(seeds[3], 71), 0)
    return {"sources": sources, "blocks": blocks, "pattern": pattern}


def layer_apply(vector, layer_blocks, layer_pattern, row_ids):
    width = layer_blocks.shape[-1]
    half_width = width // 2
    tiles = vector.reshape(vector.shape[0], -1, width)
    column_ids = jnp.concatenate([row_ids[:, None], layer_pattern.astype(jnp.int32)], axis=1)
    picked = jnp.take(tiles, column_ids, axis=1)
    real_in = jnp.concatenate([picked[..., :half_width], -picked[..., half_width:]], axis=-1)
    imag_in = jnp.concatenate([picked[..., half_width:], picked[..., :half_width]], axis=-1)
    mats = layer_blocks.astype(jnp.float32)
    real_out = jnp.einsum("rbkc,bkoc->rbo", real_in.astype(jnp.float32), mats)
    imag_out = jnp.einsum("rbkc,bkoc->rbo", imag_in.astype(jnp.float32), mats)
    return jnp.concatenate([real_out, imag_out], axis=-1).reshape(vector.shape[0], -1)


def reference(sources, blocks, pattern):
    row_ids = jnp.arange(NBLK, dtype=jnp.int32)
    start = jnp.zeros(sources.shape[1:], jnp.float32)
    seg_layers = SEG * LAY_DEV
    layer_ids = jnp.arange(LAYERS, dtype=jnp.int32)
    position = (layer_ids + seg_layers // 2) % seg_layers
    keep_down = (position != 0).astype(jnp.float32)
    keep_up = (position != seg_layers - 1).astype(jnp.float32)

    def descend(front_val, inputs):
        layer_src, layer_blocks, layer_pattern, keep = inputs
        summed = (layer_src + front_val * keep).astype(jnp.bfloat16)
        result = layer_apply(summed, layer_blocks, layer_pattern, row_ids)
        return result, result

    _, down = lax.scan(descend, start, (sources, blocks, pattern, keep_down))

    def ascend(front_val, inputs):
        layer_down, layer_blocks, layer_pattern, keep = inputs
        result = layer_down + layer_apply((front_val * keep).astype(jnp.bfloat16), layer_blocks, layer_pattern, row_ids)
        return result, result

    _, upper = lax.scan(ascend, start, (down, blocks, pattern, keep_up), reverse=True)
    return upper
```

```python
import functools

import jax
import jax.numpy as jnp
from jax import lax
from jax.experimental import pallas as pl
from jax.experimental.pallas import tpu as pltpu
from jax.sharding import PartitionSpec as P

SEG = 4
AXES = ("sweep", "tile")


def swap_route(pairs, sweeps, tiles, flip):
    route = []
    for layer in range(sweeps):
        other = pairs.get(layer, layer)
        mask = flip if other != layer else (flip or 1)
        route += [(layer * tiles + t, other * tiles + (t ^ mask)) for t in range(tiles)]
    return route


def apply_kernel(pieces, with_src, stage, info, *refs):
    recs, refs = refs[:pieces], refs[pieces:]
    if with_src:
        srcs, refs = refs[: with_src], refs[with_src:]
    own_blocks, pair_blocks, state_in, state_out, msg_out, vec = refs
    nb = own_blocks.shape[0]
    width = own_blocks.shape[-1]
    half = width // 2
    lane = lax.broadcasted_iota(jnp.int32, (1, 1, width), 2)
    sign = jnp.where(lane < half, 1.0, -1.0).astype(jnp.float32)
    at = 0
    for rec in recs:
        count = rec.shape[0]
        value = rec[...].astype(jnp.float32)
        if with_src:
            src = jnp.concatenate([s[...] for s in srcs[at // nb : (at + count) // nb]], axis=0)
            value = src if stage == 0 else value + src
        value = value.astype(jnp.bfloat16).astype(jnp.float32)
        real_in = value * sign
        imag_in = pltpu.roll(value, half, axis=2)
        vec[pl.ds(at, count)] = jnp.concatenate([real_in, imag_in], axis=1).astype(jnp.bfloat16)
        at += count
    rows = 2 * nb
    active = info[rows * 4 + stage] != 0
    for row in range(rows):
        source = own_blocks if row < nb else pair_blocks
        mats = jnp.concatenate([source[row % nb, j] for j in range(4)], axis=1)
        inputs = jnp.concatenate([vec[info[row * 4 + j]] for j in range(4)], axis=1)
        out = lax.dot_general(
            inputs, mats, (((1,), (1,)), ((), ())), preferred_element_type=jnp.float32
        )
        rhs = out.shape[0] // 2
        result = jnp.concatenate([out[:rhs], out[rhs:]], axis=1)
        state = jnp.where(active, state_in[row] + result, state_in[row])
        state_out[row] = state
        msg = result if stage < SEG - 1 else state
        msg_out[row] = msg.astype(jnp.bfloat16)


def layer_apply(stage, info, recs, srcs, own_blocks, pair_blocks, state):
    nb = own_blocks.shape[0]
    total = sum(r.shape[0] for r in recs)
    rhs, width = recs[0].shape[1:]
    vmem = pl.BlockSpec(memory_space=pltpu.VMEM)
    args = [*recs, *srcs, own_blocks, pair_blocks, state]
    return pl.pallas_call(
        functools.partial(apply_kernel, len(recs), len(srcs), stage),
        in_specs=[pl.BlockSpec(memory_space=pltpu.SMEM)] + [vmem] * len(args),
        out_specs=[vmem, vmem],
        out_shape=[
            jax.ShapeDtypeStruct((2 * nb, rhs, width), jnp.float32),
            jax.ShapeDtypeStruct((2 * nb, rhs, width), jnp.bfloat16),
        ],
        scratch_shapes=[pltpu.VMEM((total, 2 * rhs, width), jnp.bfloat16)],
        name=f"apply_{stage}",
    )(info, *args)


def per_device(sources, blocks, pattern):
    sweeps, tiles = lax.axis_size("sweep"), lax.axis_size("tile")
    sweep, tile = lax.axis_index("sweep"), lax.axis_index("tile")
    own_blocks, own_pattern = blocks[0], pattern[0]
    nb, width = own_blocks.shape[0], own_blocks.shape[-1]
    rhs = sources.shape[1]

    flat = {layer: layer ^ 1 for layer in range(sweeps)}
    odd = {layer: ((layer + 1) ^ 1) - 1 for layer in range(1, sweeps - 1)}
    same = {}

    def exchange(value, pairs, flip):
        return lax.ppermute(value, AXES, swap_route(pairs, sweeps, tiles, flip))

    def own_swap(value, flip):
        return lax.ppermute(value, "tile", [(t, t ^ flip) for t in range(tiles)])

    src_own = sources[0].reshape(rhs, nb, width).transpose(1, 0, 2)
    srcs = [src_own] + [own_swap(src_own, flip) for flip in range(1, tiles)]
    pair_blocks = own_swap(own_blocks, 1)
    pair_pattern = own_swap(own_pattern, 1)

    local = jnp.arange(nb, dtype=jnp.int32)
    columns = jnp.concatenate(
        [
            jnp.concatenate([(tile ^ flip) * nb + local[:, None], pat], axis=1)
            for flip, pat in ((0, own_pattern), (1, pair_pattern))
        ],
        axis=0,
    )
    slots = ((columns // nb) ^ tile) * nb + columns % nb
    first = jnp.maximum(((sweep + SEG // 2) // SEG) * SEG - SEG // 2, 0)
    place = sweep - first
    last = ((sweep + 1) % SEG == SEG // 2) | (sweep == sweeps - 1)
    flags = [place == stage for stage in range(SEG)]
    flags += [(place == SEG - 2 - step) & ~last for step in range(SEG - 1)]
    info = jnp.concatenate([slots.reshape(-1), jnp.stack(flags).astype(jnp.int32)])

    state = jnp.zeros((2 * nb, rhs, width), jnp.float32)
    stage_pairs = [flat, odd, flat, flat, odd, flat]
    recs = srcs
    for stage in range(2 * SEG - 1):
        state, msg = layer_apply(
            stage, info, recs, srcs if stage < SEG else [], own_blocks, pair_blocks, state
        )
        if stage < 2 * SEG - 2:
            recs = [exchange(msg, stage_pairs[stage], flip) for flip in range(0, tiles, 2)]
    return state[:nb].transpose(1, 0, 2).reshape(1, rhs, nb * width)


def solution(mesh):
    return jax.shard_map(
        per_device,
        mesh=mesh,
        in_specs=(
            P("sweep", None, "tile"),
            P("sweep", "tile", None, None, None),
            P("sweep", "tile", None),
        ),
        out_specs=P("sweep", None, "tile"),
        check_vma=False,
    )
```

```python
import functools

import jax
import jax.numpy as jnp
from jax import lax
from jax.experimental import pallas as pl
from jax.experimental.pallas import tpu as pltpu
from jax.sharding import PartitionSpec as P

SEG = 4
AXES = ("sweep", "tile")


def swap_route(pairs, sweeps, tiles, flip):
    route = []
    for layer in range(sweeps):
        other = pairs.get(layer, layer)
        mask = flip if other != layer else (flip or 1)
        route += [(layer * tiles + t, other * tiles + (t ^ mask)) for t in range(tiles)]
    return route


def apply_kernel(pieces, with_src, stage, info, *refs):
    recs, refs = refs[:pieces], refs[pieces:]
    if with_src:
        srcs, refs = refs[: with_src], refs[with_src:]
    own_blocks, pair_blocks, state_in, state_out, *msg_out, vec = refs
    nb = own_blocks.shape[0]
    width = own_blocks.shape[-1]
    half = width // 2
    lane = lax.broadcasted_iota(jnp.int32, (1, 1, width), 2)
    sign = jnp.where(lane < half, 1.0, -1.0).astype(jnp.float32)
    at = 0
    for rec in recs:
        count = rec.shape[0]
        value = rec[...].astype(jnp.float32)
        if with_src:
            src = jnp.concatenate([s[...] for s in srcs[at // nb : (at + count) // nb]], axis=0)
            value = src if stage == 0 else value + src
        value = value.astype(jnp.bfloat16).astype(jnp.float32)
        real_in = value * sign
        imag_in = pltpu.roll(value, half, axis=2)
        vec[pl.ds(at, count)] = jnp.concatenate([real_in, imag_in], axis=1).astype(jnp.bfloat16)
        at += count
    rows = 2 * nb if msg_out else nb
    active = info[8 * nb + stage] != 0
    for row in range(rows):
        source = own_blocks if row < nb else pair_blocks
        mats = jnp.concatenate([source[row % nb, j] for j in range(4)], axis=1)
        inputs = jnp.concatenate([vec[info[row * 4 + j]] for j in range(4)], axis=1)
        out = lax.dot_general(
            inputs, mats, (((1,), (1,)), ((), ())), preferred_element_type=jnp.float32
        )
        rhs = out.shape[0] // 2
        result = jnp.concatenate([out[:rhs], out[rhs:]], axis=1)
        state = jnp.where(active, state_in[row] + result, state_in[row])
        if not msg_out:
            state_out[:, row * width : (row + 1) * width] = state
            continue
        state_out[row] = state
        msg = result if stage < SEG - 1 else state
        msg_out[0][row] = msg.astype(jnp.bfloat16)


def layer_apply(stage, info, recs, srcs, own_blocks, pair_blocks, state):
    nb = own_blocks.shape[0]
    total = sum(r.shape[0] for r in recs)
    rhs, width = recs[0].shape[1:]
    vmem = pl.BlockSpec(memory_space=pltpu.VMEM)
    args = [*recs, *srcs, own_blocks, pair_blocks, state]
    out_shape = [
        jax.ShapeDtypeStruct((2 * nb, rhs, width), jnp.float32),
        jax.ShapeDtypeStruct((2 * nb, rhs, width), jnp.bfloat16),
    ]
    if stage == 2 * SEG - 2:
        out_shape = [jax.ShapeDtypeStruct((rhs, nb * width), jnp.float32)]
    return pl.pallas_call(
        functools.partial(apply_kernel, len(recs), len(srcs), stage),
        in_specs=[pl.BlockSpec(memory_space=pltpu.SMEM)] + [vmem] * len(args),
        out_specs=[vmem] * len(out_shape),
        out_shape=out_shape,
        scratch_shapes=[pltpu.VMEM((total, 2 * rhs, width), jnp.bfloat16)],
        compiler_params=pltpu.CompilerParams(vmem_limit_bytes=8 * 1024 * 1024),
        name=f"apply_{stage}",
    )(info, *args)


def per_device(sources, blocks, pattern):
    sweeps, tiles = lax.axis_size("sweep"), lax.axis_size("tile")
    sweep, tile = lax.axis_index("sweep"), lax.axis_index("tile")
    own_blocks, own_pattern = blocks[0], pattern[0]
    nb, width = own_blocks.shape[0], own_blocks.shape[-1]
    rhs = sources.shape[1]

    flat = {layer: layer ^ 1 for layer in range(sweeps)}
    odd = {layer: ((layer + 1) ^ 1) - 1 for layer in range(1, sweeps - 1)}

    def exchange(value, pairs, flip):
        return lax.ppermute(value, AXES, swap_route(pairs, sweeps, tiles, flip))

    def own_swap(value, flip):
        return lax.ppermute(value, "tile", [(t, t ^ flip) for t in range(tiles)])

    src_own = sources[0].reshape(rhs, nb, width).transpose(1, 0, 2)
    srcs = [src_own] + [own_swap(src_own, flip) for flip in range(1, tiles)]
    pair_blocks = own_swap(own_blocks, 1)
    pair_pattern = own_swap(own_pattern, 1)

    local = jnp.arange(nb, dtype=jnp.int32)
    columns = jnp.concatenate(
        [
            jnp.concatenate([(tile ^ flip) * nb + local[:, None], pat], axis=1)
            for flip, pat in ((0, own_pattern), (1, pair_pattern))
        ],
        axis=0,
    )
    slots = ((columns // nb) ^ tile) * nb + columns % nb
    first = jnp.maximum(((sweep + SEG // 2) // SEG) * SEG - SEG // 2, 0)
    place = sweep - first
    last = ((sweep + 1) % SEG == SEG // 2) | (sweep == sweeps - 1)
    flags = [place == stage for stage in range(SEG)]
    flags += [(place == SEG - 2 - step) & ~last for step in range(SEG - 1)]
    info = jnp.concatenate([slots.reshape(-1), jnp.stack(flags).astype(jnp.int32)])

    state = jnp.zeros((2 * nb, rhs, width), jnp.float32)
    stage_pairs = [flat, odd, flat, flat, odd, flat]
    recs = srcs
    for stage in range(2 * SEG - 1):
        state, *msg = layer_apply(
            stage, info, recs, srcs if stage < SEG else [], own_blocks, pair_blocks, state
        )
        if msg:
            recs = [exchange(msg[0], stage_pairs[stage], flip) for flip in range(0, tiles, 2)]
    return state[None]


def solution(mesh):
    return jax.shard_map(
        per_device,
        mesh=mesh,
        in_specs=(
            P("sweep", None, "tile"),
            P("sweep", "tile", None, None, None),
            P("sweep", "tile", None),
        ),
        out_specs=P("sweep", None, "tile"),
        check_vma=False,
    )
```

```python
import functools

import jax
import jax.numpy as jnp
from jax import lax
from jax.experimental import pallas as pl
from jax.experimental.pallas import tpu as pltpu
from jax.sharding import PartitionSpec as P


SEG = 4
AXES = ("sweep", "tile")
VMEM = pl.BlockSpec(memory_space=pltpu.VMEM)
SMEM = pl.BlockSpec(memory_space=pltpu.SMEM)


def place_of(sweep):
    turn = lax.rem(sweep + SEG // 2, SEG)
    return jnp.where(sweep < SEG // 2, sweep, turn)


def apply_kernel(stage, plan, *refs):
    rec_flips, add_src, row_flips, block_rows, n_states, has_msg, keep_src = plan
    refs = list(refs)
    take = lambda n: [refs.pop(0) for _ in range(n)]
    (patterns,), recs, srcs = take(1), take(len(rec_flips)), take(int(add_src))
    blocks, states = take(len(block_rows)), take(n_states)
    state_out = refs.pop(0)
    msg_out = refs.pop(0) if has_msg else None
    src_out = refs.pop(0) if keep_src else None
    (vec,) = refs
    width = blocks[0].shape[-1]
    half = width // 2
    off, nb = patterns.shape[0] // 3, patterns.shape[1]
    base = lax.axis_index("tile") * nb
    place = place_of(lax.axis_index("sweep"))
    lane = lax.broadcasted_iota(jnp.int32, (1, 1, width), 2)
    sign = jnp.where(lane < half, 1.0, -1.0).astype(jnp.float32)
    for rec, flips in zip(recs, rec_flips):
        for index, flip in enumerate(flips):
            value = rec[pl.ds(index * nb, nb)].astype(jnp.float32)
            slots = pl.ds(flip * nb, nb)
            if keep_src:
                src_out[slots] = value
            if add_src:
                value = value + srcs[0][slots]
            value = value.astype(jnp.bfloat16).astype(jnp.float32)
            imag_in = pltpu.roll(value, half, axis=2)
            pair = jnp.concatenate([value * sign, imag_in], axis=1)
            vec[slots] = pair.astype(jnp.bfloat16)
    row_refs = [(ref, at) for ref, count in zip(blocks, block_rows) for at in range(count)]
    for row, (ref, at) in enumerate(row_refs):
        group, local = divmod(row, nb)
        flip = row_flips[group]
        slots = [flip * nb + local]
        slots += [patterns[flip * off + j, local] ^ base for j in range(off)]
        mats = jnp.concatenate([ref[at, j] for j in range(off + 1)], axis=1)
        inputs = jnp.concatenate([vec[slot] for slot in slots], axis=1)
        out = lax.dot_general(
            inputs, mats, (((1,), (1,)), ((), ())), preferred_element_type=jnp.float32
        )
        rhs = out.shape[0] // 2
        result = jnp.concatenate([out[:rhs], out[rhs:]], axis=1)
        if stage == 4:
            result = states[group][local] + result
        if stage == 5:
            sweep = lax.axis_index("sweep")
            inner = (sweep >= SEG // 2) & (sweep < lax.axis_size("sweep") - SEG // 2)
            result = states[group][local] + jnp.where(inner, result, 0.0)
        if stage == 6:
            result = states[0][row] + result
            for other in (1, 2, 3):
                result = jnp.where(place == other, states[other][row], result)
            state_out[:, row * width : (row + 1) * width] = result
            continue
        if row < state_out.shape[0]:
            state_out[row] = result
        msg_out[row] = result.astype(jnp.bfloat16)


def layer_apply(stage, patterns, row_flips, recs, blocks, src=None, states=(), keep_src=False):
    arrays = [r for r, _ in recs]
    nb = patterns.shape[1]
    rhs, width = arrays[0].shape[1:]
    total = sum(r.shape[0] for r in arrays)
    rows = sum(b.shape[0] for b in blocks)
    has_msg = stage < 2 * SEG - 2
    if has_msg:
        kept = nb if stage < 3 else rows
        out_shape = [
            jax.ShapeDtypeStruct((kept, rhs, width), jnp.float32),
            jax.ShapeDtypeStruct((rows, rhs, width), jnp.bfloat16),
        ]
        if keep_src:
            out_shape.append(jax.ShapeDtypeStruct((total, rhs, width), jnp.float32))
    else:
        out_shape = [jax.ShapeDtypeStruct((rhs, rows * width), jnp.float32)]
    plan = (
        tuple(tuple(f) for _, f in recs),
        src is not None,
        tuple(row_flips),
        tuple(b.shape[0] for b in blocks),
        len(states),
        has_msg,
        keep_src,
    )
    args = [*arrays, *([] if src is None else [src]), *blocks, *states]
    return pl.pallas_call(
        functools.partial(apply_kernel, stage, plan),
        in_specs=[SMEM] + [VMEM] * len(args),
        out_specs=[VMEM] * len(out_shape),
        out_shape=out_shape,
        scratch_shapes=[pltpu.VMEM((total, 2 * rhs, width), jnp.bfloat16)],
        compiler_params=pltpu.CompilerParams(vmem_limit_bytes=8 * 1024 * 1024),
    )(patterns, *args)


def stage_in(blocks):
    def kernel(source, out, sem):
        copy = pltpu.make_async_copy(source, out, sem)
        copy.start()
        copy.wait()

    return pl.pallas_call(
        kernel,
        in_specs=[pl.BlockSpec(memory_space=pl.ANY)],
        out_specs=VMEM,
        out_shape=jax.ShapeDtypeStruct(blocks.shape, blocks.dtype),
        scratch_shapes=[pltpu.SemaphoreType.DMA(())],
        compiler_params=pltpu.CompilerParams(vmem_limit_bytes=4 * 1024 * 1024),
        name="stage_in",
    )(blocks)


def per_device(sources, blocks, pattern):
    sweeps, tiles = lax.axis_size("sweep"), lax.axis_size("tile")
    own_blocks, own_pattern = blocks[0], pattern[0].T
    nb, width = own_blocks.shape[0], own_blocks.shape[-1]
    rhs, hn = sources.shape[1], nb // 2
    layers = range(sweeps)

    def place(layer):
        return layer if layer < SEG // 2 else (layer + SEG // 2) % SEG

    def plane_late(layer):
        return (layer + SEG // 2) % SEG >= 2

    everyone = {layer: layer for layer in layers}
    early = {layer: layer for layer in layers if not plane_late(layer)}
    late = {layer: layer for layer in layers if plane_late(layer)}
    late_y = {layer: layer ^ 1 for layer in late}
    starts = {layer: layer for layer in layers if place(layer) < 2}
    start_y = {layer: layer ^ 1 for layer in layers if place(layer) < 2}
    across_y = {layer: layer ^ 1 for layer in layers}
    across_z = {
        layer: layer + (2 if not plane_late(layer) else -2)
        for layer in range(SEG // 2, sweeps - SEG // 2)
    }
    core_flips = [f for f in range(tiles) if not f & 2]
    even_flips = [f for f in range(tiles) if not f & 1]

    def swap(value, pairs, flip):
        route = []
        for layer in layers:
            mask = flip if layer in pairs else 1
            other = pairs.get(layer, layer)
            route += [(layer * tiles + t, other * tiles + (t ^ mask)) for t in range(tiles)]
        return lax.ppermute(value, AXES, route)

    def hop(msg, pairs, flips, other, own=False):
        recs = [(msg, (0, other))] if own else []
        for f in flips:
            if f or not own:
                recs.append((swap(msg, pairs, f), (f, f ^ other)))
        return recs

    src_own = sources[0].reshape(rhs, nb, width).transpose(1, 0, 2)
    src_pieces = [(src_own, (0,))]
    src_pieces += [(swap(src_own, everyone, f), (f,)) for f in range(1, tiles)]
    core_blocks = swap(own_blocks, everyone, 1)
    core_pattern = swap(own_pattern, everyone, 1)
    x_pattern = swap(own_pattern, everyone, 2)
    y_blocks = swap(own_blocks, late_y, 0)
    x_blocks = swap(own_blocks, late, 2)
    own = stage_in(own_blocks)

    patterns = jnp.concatenate([own_pattern, core_pattern, x_pattern], axis=0)
    core_rows = dict(patterns=patterns, row_flips=(0, 1))
    down_0, msg, src_all = layer_apply(
        0, recs=src_pieces, blocks=[own, core_blocks], keep_src=True, **core_rows
    )
    recs = hop(msg, start_y, even_flips, 1)

    y_patterns = swap(patterns, late_y, 0)
    src_other = swap(src_all, late_y, 0)
    diag_0 = swap(y_blocks[:hn], late, 2)
    diag_1 = swap(x_blocks[hn:], late_y, 0)

    down_1, msg = layer_apply(
        1, recs=recs, blocks=[own, core_blocks], src=src_all, **core_rows
    )
    recs = hop(msg, across_z, even_flips, 1)
    down_1_x = swap(down_1, starts, 2)
    x_late = swap(own_blocks, early, 2)

    y_core = swap(y_blocks, everyone, 1)
    down_2, msg = layer_apply(2, y_patterns, (0, 1), recs, [y_blocks, y_core], src=src_other)
    recs = hop(msg, late, even_flips, 1, own=True)
    down_2_x = swap(down_2, late, 2)
    own_rows = dict(patterns=patterns, row_flips=(0, 2))
    down_3, msg = layer_apply(
        3, recs=recs, blocks=[own, x_blocks], src=src_all, **own_rows
    )
    recs = hop(msg, everyone, core_flips, 2, own=True)
    up_2, msg = layer_apply(
        4, y_patterns, (0, 2), recs, [y_blocks, diag_0, diag_1], states=[down_2, down_2_x]
    )
    recs = hop(msg, across_z, core_flips, 2)
    up_2_own = swap(up_2[:nb], late_y, 0)
    up_1, msg = layer_apply(
        5, recs=recs, blocks=[own, x_late], states=[down_1, down_1_x], **own_rows
    )
    recs = hop(msg, across_y, core_flips, 2)
    (upper,) = layer_apply(
        6,
        patterns=patterns,
        row_flips=(0,),
        recs=recs,
        blocks=[own],
        states=[down_0, up_1, up_2_own, down_3],
    )
    return upper[None]


def solution(mesh):
    return jax.shard_map(
        per_device,
        mesh=mesh,
        in_specs=(
            P("sweep", None, "tile"),
            P("sweep", "tile", None, None, None),
            P("sweep", "tile", None),
        ),
        out_specs=P("sweep", None, "tile"),
        check_vma=False,
    )
```

```python
import functools

import jax
import jax.numpy as jnp
from jax import lax
from jax.experimental import pallas as pl
from jax.experimental.pallas import tpu as pltpu
from jax.sharding import PartitionSpec as P


SEG = 4
AXES = ("sweep", "tile")
VMEM = pl.BlockSpec(memory_space=pltpu.VMEM)
SMEM = pl.BlockSpec(memory_space=pltpu.SMEM)


def place_of(sweep):
    turn = lax.rem(sweep + SEG // 2, SEG)
    return jnp.where(sweep < SEG // 2, sweep, turn)


def apply_kernel(stage, plan, *refs):
    rec_flips, add_src, row_flips, block_rows, n_states, has_msg, keep_src = plan
    refs = list(refs)
    take = lambda n: [refs.pop(0) for _ in range(n)]
    (patterns,), recs, srcs = take(1), take(len(rec_flips)), take(int(add_src))
    blocks, states = take(len(block_rows)), take(n_states)
    state_out = refs.pop(0)
    msg_out = refs.pop(0) if has_msg else None
    src_out = refs.pop(0) if keep_src else None
    (vec,) = refs
    width = blocks[0].shape[-1]
    half = width // 2
    off, nb = patterns.shape[0] // 2, patterns.shape[1]
    base = lax.axis_index("tile") * nb
    place = place_of(lax.axis_index("sweep"))
    lane = lax.broadcasted_iota(jnp.int32, (1, 1, width), 2)
    sign = jnp.where(lane < half, 1.0, -1.0).astype(jnp.float32)
    for rec, flips in zip(recs, rec_flips):
        for index, flip in enumerate(flips):
            value = rec[pl.ds(index * nb, nb)].astype(jnp.float32)
            slots = pl.ds(flip * nb, nb)
            if keep_src:
                src_out[slots] = value
            if add_src:
                value = value + srcs[0][slots]
            value = value.astype(jnp.bfloat16).astype(jnp.float32)
            imag_in = pltpu.roll(value, half, axis=2)
            pair = jnp.concatenate([value * sign, imag_in], axis=1)
            vec[slots] = pair.astype(jnp.bfloat16)
    row_refs = [(ref, at) for ref, count in zip(blocks, block_rows) for at in range(count)]
    for row, (ref, at) in enumerate(row_refs):
        group, local = divmod(row, nb)
        flip = row_flips[group]
        slots = [flip * nb + local]
        slots += [patterns[group * off + j, local] ^ base for j in range(off)]
        mats = jnp.concatenate([ref[at, j] for j in range(off + 1)], axis=1)
        inputs = jnp.concatenate([vec[slot] for slot in slots], axis=1)
        out = lax.dot_general(
            inputs, mats, (((1,), (1,)), ((), ())), preferred_element_type=jnp.float32
        )
        rhs = out.shape[0] // 2
        result = jnp.concatenate([out[:rhs], out[rhs:]], axis=1)
        if stage == 4:
            result = states[0][row] + result
        if stage == 5:
            sweep = lax.axis_index("sweep")
            inner = (sweep >= SEG // 2) & (sweep < lax.axis_size("sweep") - SEG // 2)
            result = states[group][local] + jnp.where(inner, result, 0.0)
        if stage == 6:
            result = states[0][row] + result
            for other in (1, 2, 3):
                result = jnp.where(place == other, states[other][row], result)
            state_out[:, row * width : (row + 1) * width] = result
            continue
        if row < state_out.shape[0]:
            state_out[row] = result
        msg_out[row] = result.astype(jnp.bfloat16)


def layer_apply(stage, patterns, row_flips, recs, blocks, src=None, states=(), keep_src=False):
    arrays = [r for r, _ in recs]
    nb = patterns.shape[1]
    rhs, width = arrays[0].shape[1:]
    total = sum(r.shape[0] for r in arrays)
    rows = sum(b.shape[0] for b in blocks)
    has_msg = stage < 2 * SEG - 2
    if has_msg:
        kept = nb if stage < 2 else rows
        out_shape = [
            jax.ShapeDtypeStruct((kept, rhs, width), jnp.float32),
            jax.ShapeDtypeStruct((rows, rhs, width), jnp.bfloat16),
        ]
        if keep_src:
            out_shape.append(jax.ShapeDtypeStruct((total, rhs, width), jnp.float32))
    else:
        out_shape = [jax.ShapeDtypeStruct((rhs, rows * width), jnp.float32)]
    plan = (
        tuple(tuple(f) for _, f in recs),
        src is not None,
        tuple(row_flips),
        tuple(b.shape[0] for b in blocks),
        len(states),
        has_msg,
        keep_src,
    )
    args = [*arrays, *([] if src is None else [src]), *blocks, *states]
    return pl.pallas_call(
        functools.partial(apply_kernel, stage, plan),
        in_specs=[SMEM] + [VMEM] * len(args),
        out_specs=[VMEM] * len(out_shape),
        out_shape=out_shape,
        scratch_shapes=[pltpu.VMEM((total, 2 * rhs, width), jnp.bfloat16)],
        compiler_params=pltpu.CompilerParams(vmem_limit_bytes=8 * 1024 * 1024),
    )(patterns, *args)


def stage_in(blocks):
    def kernel(source, out, sem):
        copy = pltpu.make_async_copy(source, out, sem)
        copy.start()
        copy.wait()

    return pl.pallas_call(
        kernel,
        in_specs=[pl.BlockSpec(memory_space=pl.ANY)],
        out_specs=VMEM,
        out_shape=jax.ShapeDtypeStruct(blocks.shape, blocks.dtype),
        scratch_shapes=[pltpu.SemaphoreType.DMA(())],
        compiler_params=pltpu.CompilerParams(vmem_limit_bytes=4 * 1024 * 1024),
        name="stage_in",
    )(blocks)


def per_device(sources, blocks, pattern):
    sweeps, tiles = lax.axis_size("sweep"), lax.axis_size("tile")
    own_blocks, own_pattern = blocks[0], pattern[0].T
    nb, width = own_blocks.shape[0], own_blocks.shape[-1]
    rhs = sources.shape[1]
    layers = range(sweeps)

    def place(layer):
        return layer if layer < SEG // 2 else (layer + SEG // 2) % SEG

    def plane_late(layer):
        return (layer + SEG // 2) % SEG >= 2

    everyone = {layer: layer for layer in layers}
    early = {layer: layer for layer in layers if not plane_late(layer)}
    late = {layer: layer for layer in layers if plane_late(layer)}
    late_y = {layer: layer ^ 1 for layer in late}
    starts = {layer: layer for layer in layers if place(layer) < 2}
    start_y = {layer: layer ^ 1 for layer in layers if place(layer) < 2}
    across_y = {layer: layer ^ 1 for layer in layers}
    across_z = {
        layer: layer + (2 if not plane_late(layer) else -2)
        for layer in range(SEG // 2, sweeps - SEG // 2)
    }
    core_flips = [f for f in range(tiles) if not f & 2]
    even_flips = [f for f in range(tiles) if not f & 1]

    def swap(value, pairs, flip):
        route = []
        for layer in layers:
            mask = flip if layer in pairs else 1
            other = pairs.get(layer, layer)
            route += [(layer * tiles + t, other * tiles + (t ^ mask)) for t in range(tiles)]
        return lax.ppermute(value, AXES, route)

    def hop(msg, pairs, flips, other, own=False):
        recs = [(msg, (0, other))] if own else []
        for f in flips:
            if f or not own:
                recs.append((swap(msg, pairs, f), (f, f ^ other)))
        return recs

    src_own = sources[0].reshape(rhs, nb, width).transpose(1, 0, 2)
    src_pieces = [(src_own, (0,))]
    src_pieces += [(swap(src_own, everyone, f), (f,)) for f in range(1, tiles)]
    core_blocks = swap(own_blocks, everyone, 1)
    core_pattern = swap(own_pattern, everyone, 1)
    core_patterns = jnp.concatenate([own_pattern, core_pattern], axis=0)
    y_blocks = swap(own_blocks, late_y, 0)
    x_blocks = swap(own_blocks, late, 2)
    own = stage_in(own_blocks)

    core_rows = dict(patterns=core_patterns, row_flips=(0, 1))
    down_0, msg, src_all = layer_apply(
        0, recs=src_pieces, blocks=[own, core_blocks], keep_src=True, **core_rows
    )
    recs = hop(msg, start_y, even_flips, 1)

    y_patterns = swap(core_patterns, late_y, 0)
    src_other = swap(src_all, late_y, 0)
    later_pattern = lax.optimization_barrier((own_pattern, msg))[0]
    x_pattern = swap(later_pattern, everyone, 2)
    x_patterns = jnp.concatenate([later_pattern, x_pattern], axis=0)

    down_1, msg = layer_apply(
        1, recs=recs, blocks=[own, core_blocks], src=src_all, **core_rows
    )
    recs = hop(msg, across_z, even_flips, 1)
    y_core = swap(y_blocks, everyone, 1)
    down_1_x = swap(down_1, starts, 2)
    x_late = swap(own_blocks, early, 2)

    other_rows = dict(patterns=y_patterns, row_flips=(0, 1), blocks=[y_blocks, y_core])
    x_rows = dict(patterns=x_patterns, row_flips=(0, 2))
    down_2, msg = layer_apply(2, recs=recs, src=src_other, **other_rows)
    recs = hop(msg, late, even_flips, 1, own=True)
    down_3, msg = layer_apply(3, recs=recs, blocks=[own, x_blocks], src=src_all, **x_rows)
    recs = hop(msg, everyone, core_flips, 2, own=True)
    up_2, msg = layer_apply(4, recs=recs, states=[down_2], **other_rows)
    recs = hop(msg, across_z, even_flips, 1)
    up_2_own = swap(up_2[:nb], late_y, 0)
    up_1, msg = layer_apply(
        5, recs=recs, blocks=[own, x_late], states=[down_1, down_1_x], **x_rows
    )
    recs = hop(msg, across_y, core_flips, 2)
    (upper,) = layer_apply(
        6,
        patterns=core_patterns,
        row_flips=(0,),
        recs=recs,
        blocks=[own],
        states=[down_0, up_1, up_2_own, down_3],
    )
    return upper[None]


def solution(mesh):
    return jax.shard_map(
        per_device,
        mesh=mesh,
        in_specs=(
            P("sweep", None, "tile"),
            P("sweep", "tile", None, None, None),
            P("sweep", "tile", None),
        ),
        out_specs=P("sweep", None, "tile"),
        check_vma=False,
    )
```

```python
import functools

import jax
import jax.numpy as jnp
from jax import lax
from jax.experimental import pallas as pl
from jax.experimental.pallas import tpu as pltpu
from jax.sharding import PartitionSpec as P


SEG = 4
AXES = ("sweep", "tile")
VMEM = pl.BlockSpec(memory_space=pltpu.VMEM)
SMEM = pl.BlockSpec(memory_space=pltpu.SMEM)


def place_of(sweep):
    turn = lax.rem(sweep + SEG // 2, SEG)
    return jnp.where(sweep < SEG // 2, sweep, turn)


def apply_kernel(stage, plan, *refs):
    rec_flips, add_src, row_flips, block_rows, n_states, has_msg, keep_src = plan
    refs = list(refs)
    take = lambda n: [refs.pop(0) for _ in range(n)]
    (patterns,), recs, srcs = take(1), take(len(rec_flips)), take(int(add_src))
    blocks, states = take(len(block_rows)), take(n_states)
    state_out = refs.pop(0)
    msg_out = refs.pop(0) if has_msg else None
    src_out = refs.pop(0) if keep_src else None
    (vec,) = refs
    width = blocks[0].shape[-1]
    half = width // 2
    off, nb = patterns.shape[0] // 2, patterns.shape[1]
    columns = patterns[...] ^ (lax.axis_index("tile") * nb)
    place = place_of(lax.axis_index("sweep"))
    lane = lax.broadcasted_iota(jnp.int32, (1, 1, width), 2)
    sign = jnp.where(lane < half, 1.0, -1.0).astype(jnp.float32)
    for rec, flips in zip(recs, rec_flips):
        for index, flip in enumerate(flips):
            value = rec[pl.ds(index * nb, nb)].astype(jnp.float32)
            slots = pl.ds(flip * nb, nb)
            if keep_src:
                src_out[slots] = value
            if add_src:
                value = value + srcs[0][slots]
            value = value.astype(jnp.bfloat16).astype(jnp.float32)
            imag_in = pltpu.roll(value, half, axis=2)
            pair = jnp.concatenate([value * sign, imag_in], axis=1)
            vec[slots] = pair.astype(jnp.bfloat16)
    row_refs = [(ref, at) for ref, count in zip(blocks, block_rows) for at in range(count)]
    for row, (ref, at) in enumerate(row_refs):
        group, local = divmod(row, nb)
        flip = row_flips[group]
        slots = [flip * nb + local]
        slots += [columns[group * off + j, local] for j in range(off)]
        mats = jnp.concatenate([ref[at, j] for j in range(off + 1)], axis=1)
        inputs = jnp.concatenate([vec[slot] for slot in slots], axis=1)
        out = lax.dot_general(
            inputs, mats, (((1,), (1,)), ((), ())), preferred_element_type=jnp.float32
        )
        rhs = out.shape[0] // 2
        result = jnp.concatenate([out[:rhs], out[rhs:]], axis=1)
        if stage == 4:
            result = states[0][row] + result
        if stage == 5:
            sweep = lax.axis_index("sweep")
            inner = (sweep >= SEG // 2) & (sweep < lax.axis_size("sweep") - SEG // 2)
            result = states[group][local] + jnp.where(inner, result, 0.0)
        if stage == 6:
            result = states[0][row] + result
            for other in (1, 2, 3):
                result = jnp.where(place == other, states[other][row], result)
            state_out[:, row * width : (row + 1) * width] = result
            continue
        if row < state_out.shape[0]:
            state_out[row] = result
        msg_out[row] = result.astype(jnp.bfloat16)


def layer_apply(stage, patterns, row_flips, recs, blocks, src=None, states=(), keep_src=False):
    arrays = [r for r, _ in recs]
    nb = patterns.shape[1]
    rhs, width = arrays[0].shape[1:]
    total = sum(r.shape[0] for r in arrays)
    rows = sum(b.shape[0] for b in blocks)
    has_msg = stage < 2 * SEG - 2
    if has_msg:
        kept = nb if stage < 2 else rows
        out_shape = [
            jax.ShapeDtypeStruct((kept, rhs, width), jnp.float32),
            jax.ShapeDtypeStruct((rows, rhs, width), jnp.bfloat16),
        ]
        if keep_src:
            out_shape.append(jax.ShapeDtypeStruct((total, rhs, width), jnp.float32))
    else:
        out_shape = [jax.ShapeDtypeStruct((rhs, rows * width), jnp.float32)]
    plan = (
        tuple(tuple(f) for _, f in recs),
        src is not None,
        tuple(row_flips),
        tuple(b.shape[0] for b in blocks),
        len(states),
        has_msg,
        keep_src,
    )
    args = [*arrays, *([] if src is None else [src]), *blocks, *states]
    return pl.pallas_call(
        functools.partial(apply_kernel, stage, plan),
        in_specs=[VMEM] * (1 + len(args)),
        out_specs=[VMEM] * len(out_shape),
        out_shape=out_shape,
        scratch_shapes=[pltpu.VMEM((total, 2 * rhs, width), jnp.bfloat16)],
        compiler_params=pltpu.CompilerParams(vmem_limit_bytes=8 * 1024 * 1024),
    )(patterns, *args)


def stage_in(blocks):
    def kernel(source, out, sem):
        copy = pltpu.make_async_copy(source, out, sem)
        copy.start()
        copy.wait()

    return pl.pallas_call(
        kernel,
        in_specs=[pl.BlockSpec(memory_space=pl.ANY)],
        out_specs=VMEM,
        out_shape=jax.ShapeDtypeStruct(blocks.shape, blocks.dtype),
        scratch_shapes=[pltpu.SemaphoreType.DMA(())],
        compiler_params=pltpu.CompilerParams(vmem_limit_bytes=4 * 1024 * 1024),
        name="stage_in",
    )(blocks)


def per_device(sources, blocks, pattern):
    sweeps, tiles = lax.axis_size("sweep"), lax.axis_size("tile")
    own_blocks, own_pattern = blocks[0], pattern[0].T
    nb, width = own_blocks.shape[0], own_blocks.shape[-1]
    rhs = sources.shape[1]
    layers = range(sweeps)

    def place(layer):
        return layer if layer < SEG // 2 else (layer + SEG // 2) % SEG

    def plane_late(layer):
        return (layer + SEG // 2) % SEG >= 2

    everyone = {layer: layer for layer in layers}
    early = {layer: layer for layer in layers if not plane_late(layer)}
    late = {layer: layer for layer in layers if plane_late(layer)}
    late_y = {layer: layer ^ 1 for layer in late}
    starts = {layer: layer for layer in layers if place(layer) < 2}
    start_y = {layer: layer ^ 1 for layer in layers if place(layer) < 2}
    across_y = {layer: layer ^ 1 for layer in layers}
    across_z = {
        layer: layer + (2 if not plane_late(layer) else -2)
        for layer in range(SEG // 2, sweeps - SEG // 2)
    }
    core_flips = [f for f in range(tiles) if not f & 2]
    even_flips = [f for f in range(tiles) if not f & 1]

    def swap(value, pairs, flip):
        route = []
        for layer in layers:
            mask = flip if layer in pairs else 1
            other = pairs.get(layer, layer)
            route += [(layer * tiles + t, other * tiles + (t ^ mask)) for t in range(tiles)]
        return lax.ppermute(value, AXES, route)

    def hop(msg, pairs, flips, other, own=False):
        recs = [(msg, (0, other))] if own else []
        for f in flips:
            if f or not own:
                recs.append((swap(msg, pairs, f), (f, f ^ other)))
        return recs

    src_own = sources[0].reshape(rhs, nb, width).transpose(1, 0, 2)
    src_pieces = [(src_own, (0,))]
    src_pieces += [(swap(src_own, everyone, f), (f,)) for f in range(1, tiles)]
    core_blocks = swap(own_blocks, everyone, 1)
    core_pattern = swap(own_pattern, everyone, 1)
    core_patterns = jnp.concatenate([own_pattern, core_pattern], axis=0)
    y_blocks = swap(own_blocks, late_y, 0)
    x_blocks = swap(own_blocks, late, 2)
    own = stage_in(own_blocks)

    core_rows = dict(patterns=core_patterns, row_flips=(0, 1))
    down_0, msg, src_all = layer_apply(
        0, recs=src_pieces, blocks=[own, core_blocks], keep_src=True, **core_rows
    )
    recs = hop(msg, start_y, even_flips, 1)

    y_patterns = swap(core_patterns, late_y, 0)
    src_other = swap(src_all, late_y, 0)
    later_pattern = lax.optimization_barrier((own_pattern, msg))[0]
    x_pattern = swap(later_pattern, everyone, 2)
    x_patterns = jnp.concatenate([later_pattern, x_pattern], axis=0)

    down_1, msg = layer_apply(
        1, recs=recs, blocks=[own, core_blocks], src=src_all, **core_rows
    )
    recs = hop(msg, across_z, even_flips, 1)
    y_core = swap(y_blocks, everyone, 1)
    down_1_x = swap(down_1, starts, 2)
    x_late = swap(own_blocks, early, 2)

    other_rows = dict(patterns=y_patterns, row_flips=(0, 1), blocks=[y_blocks, y_core])
    x_rows = dict(patterns=x_patterns, row_flips=(0, 2))
    down_2, msg = layer_apply(2, recs=recs, src=src_other, **other_rows)
    recs = hop(msg, late, even_flips, 1, own=True)
    down_3, msg = layer_apply(3, recs=recs, blocks=[own, x_blocks], src=src_all, **x_rows)
    recs = hop(msg, everyone, core_flips, 2, own=True)
    up_2, msg = layer_apply(4, recs=recs, states=[down_2], **other_rows)
    recs = hop(msg, across_z, even_flips, 1)
    up_2_own = swap(up_2[:nb], late_y, 0)
    up_1, msg = layer_apply(
        5, recs=recs, blocks=[own, x_late], states=[down_1, down_1_x], **x_rows
    )
    recs = hop(msg, across_y, core_flips, 2)
    (upper,) = layer_apply(
        6,
        patterns=core_patterns,
        row_flips=(0,),
        recs=recs,
        blocks=[own],
        states=[down_0, up_1, up_2_own, down_3],
    )
    return upper[None]


def solution(mesh):
    return jax.shard_map(
        per_device,
        mesh=mesh,
        in_specs=(
            P("sweep", None, "tile"),
            P("sweep", "tile", None, None, None),
            P("sweep", "tile", None),
        ),
        out_specs=P("sweep", None, "tile"),
        check_vma=False,
    )
```

```python
import functools

import jax
import jax.numpy as jnp
from jax import lax
from jax.experimental import pallas as pl
from jax.experimental.pallas import tpu as pltpu
from jax.sharding import PartitionSpec as P


SEG = 4
AXES = ("sweep", "tile")
VMEM = pl.BlockSpec(memory_space=pltpu.VMEM)
SMEM = pl.BlockSpec(memory_space=pltpu.SMEM)


def place_of(sweep):
    turn = lax.rem(sweep + SEG // 2, SEG)
    return jnp.where(sweep < SEG // 2, sweep, turn)


def apply_kernel(stage, plan, *refs):
    rec_flips, add_src, row_flips, block_rows, n_states, has_msg, keep_src = plan
    refs = list(refs)
    take = lambda n: [refs.pop(0) for _ in range(n)]
    (patterns,), recs, srcs = take(1), take(len(rec_flips)), take(int(add_src))
    blocks, states = take(len(block_rows)), take(n_states)
    state_out = refs.pop(0)
    msg_out = refs.pop(0) if has_msg else None
    src_out = refs.pop(0) if keep_src else None
    (vec,) = refs
    width = blocks[0].shape[-1]
    half = width // 2
    off, nb = patterns.shape[0] // 2, patterns.shape[1]
    columns = patterns[...] ^ (lax.axis_index("tile") * nb)
    place = place_of(lax.axis_index("sweep"))
    lane = lax.broadcasted_iota(jnp.int32, (1, 1, width), 2)
    sign = jnp.where(lane < half, 1.0, -1.0).astype(jnp.float32)
    for rec, flips in zip(recs, rec_flips):
        for index, flip in enumerate(flips):
            value = rec[pl.ds(index * nb, nb)].astype(jnp.float32)
            slots = pl.ds(flip * nb, nb)
            if keep_src:
                src_out[slots] = value
            if add_src:
                value = value + srcs[0][slots]
            value = value.astype(jnp.bfloat16).astype(jnp.float32)
            imag_in = pltpu.roll(value, half, axis=2)
            pair = jnp.concatenate([value * sign, imag_in], axis=1)
            vec[slots] = pair.astype(jnp.bfloat16)
    row_refs = [(ref, at) for ref, count in zip(blocks, block_rows) for at in range(count)]
    for row, (ref, at) in enumerate(row_refs):
        group, local = divmod(row, nb)
        flip = row_flips[group]
        slots = [flip * nb + local]
        slots += [columns[group * off + j, local] for j in range(off)]
        mats = jnp.concatenate([ref[at, j] for j in range(off + 1)], axis=1)
        inputs = jnp.concatenate([vec[slot] for slot in slots], axis=1)
        out = lax.dot_general(
            inputs, mats, (((1,), (1,)), ((), ())), preferred_element_type=jnp.float32
        )
        rhs = out.shape[0] // 2
        result = jnp.concatenate([out[:rhs], out[rhs:]], axis=1)
        if stage == 4:
            result = states[0][row] + result
        if stage == 5:
            sweep = lax.axis_index("sweep")
            inner = (sweep >= SEG // 2) & (sweep < lax.axis_size("sweep") - SEG // 2)
            result = states[group][local] + jnp.where(inner, result, 0.0)
        if stage == 6:
            result = states[0][row] + result
            for other in (1, 2, 3):
                result = jnp.where(place == other, states[other][row], result)
            state_out[:, row * width : (row + 1) * width] = result
            continue
        if row < state_out.shape[0]:
            state_out[row] = result
        msg_out[row] = result.astype(jnp.bfloat16)


def layer_apply(stage, patterns, row_flips, recs, blocks, src=None, states=(), keep_src=False):
    arrays = [r for r, _ in recs]
    nb = patterns.shape[1]
    rhs, width = arrays[0].shape[1:]
    total = sum(r.shape[0] for r in arrays)
    rows = sum(b.shape[0] for b in blocks)
    has_msg = stage < 2 * SEG - 2
    if has_msg:
        kept = nb if stage < 2 else rows
        out_shape = [
            jax.ShapeDtypeStruct((kept, rhs, width), jnp.float32),
            jax.ShapeDtypeStruct((rows, rhs, width), jnp.bfloat16),
        ]
        if keep_src:
            out_shape.append(jax.ShapeDtypeStruct((total, rhs, width), jnp.float32))
    else:
        out_shape = [jax.ShapeDtypeStruct((rhs, rows * width), jnp.float32)]
    plan = (
        tuple(tuple(f) for _, f in recs),
        src is not None,
        tuple(row_flips),
        tuple(b.shape[0] for b in blocks),
        len(states),
        has_msg,
        keep_src,
    )
    args = [*arrays, *([] if src is None else [src]), *blocks, *states]
    return pl.pallas_call(
        functools.partial(apply_kernel, stage, plan),
        in_specs=[VMEM] * (1 + len(args)),
        out_specs=[VMEM] * len(out_shape),
        out_shape=out_shape,
        scratch_shapes=[pltpu.VMEM((total, 2 * rhs, width), jnp.bfloat16)],
        compiler_params=pltpu.CompilerParams(vmem_limit_bytes=8 * 1024 * 1024),
    )(patterns, *args)


def stage_in(blocks):
    def kernel(source, out, sem):
        copy = pltpu.make_async_copy(source, out, sem)
        copy.start()
        copy.wait()

    return pl.pallas_call(
        kernel,
        in_specs=[pl.BlockSpec(memory_space=pl.ANY)],
        out_specs=VMEM,
        out_shape=jax.ShapeDtypeStruct(blocks.shape, blocks.dtype),
        scratch_shapes=[pltpu.SemaphoreType.DMA(())],
        compiler_params=pltpu.CompilerParams(vmem_limit_bytes=4 * 1024 * 1024),
        name="stage_in",
    )(blocks)


def per_device(sources, blocks, pattern):
    sweeps, tiles = lax.axis_size("sweep"), lax.axis_size("tile")
    own_blocks, own_pattern = blocks[0], pattern[0].T
    nb, width = own_blocks.shape[0], own_blocks.shape[-1]
    rhs = sources.shape[1]
    layers = range(sweeps)

    def place(layer):
        return layer if layer < SEG // 2 else (layer + SEG // 2) % SEG

    def plane_late(layer):
        return (layer + SEG // 2) % SEG >= 2

    everyone = {layer: layer for layer in layers}
    inner = range(SEG // 2, sweeps - SEG // 2)
    early = {layer: layer for layer in inner if not plane_late(layer)}
    late = {layer: layer for layer in inner if plane_late(layer)}
    late_y = {layer: layer ^ 1 for layer in late}
    starts = {layer: layer for layer in layers if place(layer) < 2}
    start_y = {layer: layer ^ 1 for layer in layers if place(layer) < 2}
    across_y = {layer: layer ^ 1 for layer in layers}
    across_z = {layer: layer + (-2 if plane_late(layer) else 2) for layer in inner}
    core_flips = [f for f in range(tiles) if not f & 2]
    even_flips = [f for f in range(tiles) if not f & 1]

    def swap(value, pairs, flip):
        route = []
        for layer in layers:
            mask = flip if layer in pairs else 1
            other = pairs.get(layer, layer)
            route += [(layer * tiles + t, other * tiles + (t ^ mask)) for t in range(tiles)]
        return lax.ppermute(value, AXES, route)

    def hop(msg, pairs, flips, other, own=False):
        recs = [(msg, (0, other))] if own else []
        for f in flips:
            if f or not own:
                recs.append((swap(msg, pairs, f), (f, f ^ other)))
        return recs

    src_own = sources[0].reshape(rhs, nb, width).transpose(1, 0, 2)
    src_pieces = [(src_own, (0,))]
    src_pieces += [(swap(src_own, everyone, f), (f,)) for f in range(1, tiles)]
    core_blocks = swap(own_blocks, everyone, 1)
    core_pattern = swap(own_pattern, everyone, 1)
    core_patterns = jnp.concatenate([own_pattern, core_pattern], axis=0)
    y_blocks = swap(own_blocks, late_y, 0)
    x_blocks = swap(own_blocks, late, 2)
    own = stage_in(own_blocks)

    core_rows = dict(patterns=core_patterns, row_flips=(0, 1))
    down_0, msg, src_all = layer_apply(
        0, recs=src_pieces, blocks=[own, core_blocks], keep_src=True, **core_rows
    )
    recs = hop(msg, start_y, even_flips, 1)

    y_patterns = swap(core_patterns, late_y, 0)
    src_other = swap(src_all, late_y, 0)
    later_pattern = lax.optimization_barrier((own_pattern, msg))[0]
    x_pattern = swap(later_pattern, everyone, 2)
    x_patterns = jnp.concatenate([later_pattern, x_pattern], axis=0)

    down_1, msg = layer_apply(
        1, recs=recs, blocks=[own, core_blocks], src=src_all, **core_rows
    )
    recs = hop(msg, across_z, even_flips, 1)
    y_core = swap(y_blocks, everyone, 1)
    down_1_x = swap(down_1, starts, 2)
    x_late = swap(own_blocks, early, 2)

    other_rows = dict(patterns=y_patterns, row_flips=(0, 1), blocks=[y_blocks, y_core])
    x_rows = dict(patterns=x_patterns, row_flips=(0, 2))
    down_2, msg = layer_apply(2, recs=recs, src=src_other, **other_rows)
    recs = hop(msg, late, even_flips, 1, own=True)
    down_3, msg = layer_apply(3, recs=recs, blocks=[own, x_blocks], src=src_all, **x_rows)
    recs = hop(msg, everyone, core_flips, 2, own=True)
    up_2, msg = layer_apply(4, recs=recs, states=[down_2], **other_rows)
    recs = hop(msg, across_z, even_flips, 1)
    up_2_own = swap(up_2[:nb], late_y, 0)
    up_1, msg = layer_apply(
        5, recs=recs, blocks=[own, x_late], states=[down_1, down_1_x], **x_rows
    )
    recs = hop(msg, across_y, core_flips, 2)
    (upper,) = layer_apply(
        6,
        patterns=core_patterns,
        row_flips=(0,),
        recs=recs,
        blocks=[own],
        states=[down_0, up_1, up_2_own, down_3],
    )
    return upper[None]


def solution(mesh):
    return jax.shard_map(
        per_device,
        mesh=mesh,
        in_specs=(
            P("sweep", None, "tile"),
            P("sweep", "tile", None, None, None),
            P("sweep", "tile", None),
        ),
        out_specs=P("sweep", None, "tile"),
        check_vma=False,
    )
```

```python
import functools

import jax
import jax.numpy as jnp
from jax import lax
from jax.experimental import pallas as pl
from jax.experimental.pallas import tpu as pltpu
from jax.sharding import PartitionSpec as P


SEG = 4
AXES = ("sweep", "tile")
VMEM = pl.BlockSpec(memory_space=pltpu.VMEM)
SMEM = pl.BlockSpec(memory_space=pltpu.SMEM)


def place_of(sweep):
    turn = lax.rem(sweep + SEG // 2, SEG)
    return jnp.where(sweep < SEG // 2, sweep, turn)


def apply_kernel(stage, plan, *refs):
    rec_flips, add_src, row_flips, block_rows, n_states, has_msg, keep_src = plan
    refs = list(refs)
    take = lambda n: [refs.pop(0) for _ in range(n)]
    (patterns,), recs, srcs = take(1), take(len(rec_flips)), take(int(add_src))
    blocks, states = take(len(block_rows)), take(n_states)
    state_out = refs.pop(0)
    msg_out = refs.pop(0) if has_msg else None
    src_out = refs.pop(0) if keep_src else None
    (vec,) = refs
    width = blocks[0].shape[-1]
    half = width // 2
    off, nb = patterns.shape[0] // 2, patterns.shape[1]
    columns = patterns[...] ^ (lax.axis_index("tile") * nb)
    place = place_of(lax.axis_index("sweep"))
    lane = lax.broadcasted_iota(jnp.int32, (1, 1, width), 2)
    sign = jnp.where(lane < half, 1.0, -1.0).astype(jnp.float32)
    for rec, flips in zip(recs, rec_flips):
        for index, flip in enumerate(flips):
            value = rec[pl.ds(index * nb, nb)].astype(jnp.float32)
            if stage == 5:
                flip = flip ^ (2 * (lax.axis_index("tile") & 1))
            slots = pl.ds(flip * nb, nb)
            if keep_src:
                src_out[slots] = value
            if add_src:
                value = value + srcs[0][slots].astype(jnp.float32)
            value = value.astype(jnp.bfloat16).astype(jnp.float32)
            imag_in = pltpu.roll(value, half, axis=2)
            pair = jnp.concatenate([value * sign, imag_in], axis=1)
            vec[slots] = pair.astype(jnp.bfloat16)
    row_refs = [(ref, at) for ref, count in zip(blocks, block_rows) for at in range(count)]
    for row, (ref, at) in enumerate(row_refs):
        group, local = divmod(row, nb)
        flip = row_flips[group]
        slots = [flip * nb + local]
        slots += [columns[group * off + j, local] for j in range(off)]
        mats = jnp.concatenate([ref[at, j] for j in range(off + 1)], axis=1)
        inputs = jnp.concatenate([vec[slot] for slot in slots], axis=1)
        out = lax.dot_general(
            inputs, mats, (((1,), (1,)), ((), ())), preferred_element_type=jnp.float32
        )
        rhs = out.shape[0] // 2
        result = jnp.concatenate([out[:rhs], out[rhs:]], axis=1)
        if stage == 4:
            result = states[0][row] + result
        if stage == 5:
            sweep = lax.axis_index("sweep")
            inner = (sweep >= SEG // 2) & (sweep < lax.axis_size("sweep") - SEG // 2)
            result = states[group][local] + jnp.where(inner, result, 0.0)
        if stage == 6:
            result = states[0][row] + result
            for other in (1, 2, 3):
                result = jnp.where(place == other, states[other][row], result)
            state_out[:, row * width : (row + 1) * width] = result
            continue
        if row < state_out.shape[0]:
            state_out[row] = result
        msg_out[row] = result.astype(jnp.bfloat16)


def layer_apply(stage, patterns, row_flips, recs, blocks, src=None, states=(), keep_src=False):
    arrays = [r for r, _ in recs]
    nb = patterns.shape[1]
    rhs, width = arrays[0].shape[1:]
    total = sum(r.shape[0] for r in arrays)
    rows = sum(b.shape[0] for b in blocks)
    has_msg = stage < 2 * SEG - 2
    if has_msg:
        kept = nb if stage < 2 else rows
        out_shape = [
            jax.ShapeDtypeStruct((kept, rhs, width), jnp.float32),
            jax.ShapeDtypeStruct((rows, rhs, width), jnp.bfloat16),
        ]
        if keep_src:
            out_shape.append(jax.ShapeDtypeStruct((total, rhs, width), jnp.float32))
    else:
        out_shape = [jax.ShapeDtypeStruct((rhs, rows * width), jnp.float32)]
    plan = (
        tuple(tuple(f) for _, f in recs),
        src is not None,
        tuple(row_flips),
        tuple(b.shape[0] for b in blocks),
        len(states),
        has_msg,
        keep_src,
    )
    args = [*arrays, *([] if src is None else [src]), *blocks, *states]
    return pl.pallas_call(
        functools.partial(apply_kernel, stage, plan),
        in_specs=[VMEM] * (1 + len(args)),
        out_specs=[VMEM] * len(out_shape),
        out_shape=out_shape,
        scratch_shapes=[pltpu.VMEM((total, 2 * rhs, width), jnp.bfloat16)],
        compiler_params=pltpu.CompilerParams(vmem_limit_bytes=8 * 1024 * 1024),
    )(patterns, *args)


def stage_in(blocks):
    def kernel(source, out, sem):
        copy = pltpu.make_async_copy(source, out, sem)
        copy.start()
        copy.wait()

    return pl.pallas_call(
        kernel,
        in_specs=[pl.BlockSpec(memory_space=pl.ANY)],
        out_specs=VMEM,
        out_shape=jax.ShapeDtypeStruct(blocks.shape, blocks.dtype),
        scratch_shapes=[pltpu.SemaphoreType.DMA(())],
        compiler_params=pltpu.CompilerParams(vmem_limit_bytes=4 * 1024 * 1024),
        name="stage_in",
    )(blocks)


def per_device(sources, blocks, pattern):
    sweeps, tiles = lax.axis_size("sweep"), lax.axis_size("tile")
    own_blocks, own_pattern = blocks[0], pattern[0].T
    nb, width = own_blocks.shape[0], own_blocks.shape[-1]
    rhs = sources.shape[1]
    layers = range(sweeps)

    def place(layer):
        return layer if layer < SEG // 2 else (layer + SEG // 2) % SEG

    def plane_late(layer):
        return (layer + SEG // 2) % SEG >= 2

    everyone = {layer: layer for layer in layers}
    inner = range(SEG // 2, sweeps - SEG // 2)
    early = {layer: layer for layer in inner if not plane_late(layer)}
    late = {layer: layer for layer in inner if plane_late(layer)}
    late_y = {layer: layer ^ 1 for layer in late}
    starts = {layer: layer for layer in layers if place(layer) < 2}
    start_y = {layer: layer ^ 1 for layer in layers if place(layer) < 2}
    across_y = {layer: layer ^ 1 for layer in layers}
    across_z = {layer: layer + (-2 if plane_late(layer) else 2) for layer in inner if layer & 1}
    core_flips = [f for f in range(tiles) if not f & 2]
    even_flips = [f for f in range(tiles) if not f & 1]

    def swap(value, pairs, flip, odd_flip=0):
        route = []
        for layer in layers:
            for t in range(tiles):
                mask = flip ^ (odd_flip * (t & 1)) if layer in pairs else 1
                other = pairs.get(layer, layer)
                route.append((layer * tiles + t, other * tiles + (t ^ mask)))
        return lax.ppermute(value, AXES, route)

    def hop(msg, pairs, flips, other, own=False):
        recs = [(msg, (0, other))] if own else []
        for f in flips:
            if f or not own:
                recs.append((swap(msg, pairs, f), (f, f ^ other)))
        return recs

    def chip_hop(msg, pairs, other, odd_flip):
        recs = []
        for f in range(0, tiles, 4):
            far = swap(msg, pairs, f, odd_flip)
            near = swap(far, everyone, 1)
            flip = f ^ odd_flip ^ 1
            recs += [(far, (f, f ^ other)), (near, (flip, flip ^ other))]
        return recs

    src_own = sources[0].reshape(rhs, nb, width).transpose(1, 0, 2)
    src_pieces = [(src_own, (0,))]
    src_pieces += [(swap(src_own, everyone, f), (f,)) for f in range(1, tiles)]
    core_blocks = swap(own_blocks, everyone, 1)
    core_pattern = swap(own_pattern, everyone, 1)
    core_patterns = jnp.concatenate([own_pattern, core_pattern], axis=0)
    y_blocks = swap(own_blocks, late_y, 0)
    x_blocks = swap(own_blocks, late, 2)
    own = stage_in(own_blocks)

    core_rows = dict(patterns=core_patterns, row_flips=(0, 1))
    down_0, msg, src_all = layer_apply(
        0, recs=src_pieces, blocks=[own, core_blocks], keep_src=True, **core_rows
    )
    recs = hop(msg, start_y, even_flips, 1)

    y_patterns = swap(core_patterns, late_y, 0)
    src_other = swap(src_all.astype(jnp.bfloat16), late_y, 0)
    later_pattern = lax.optimization_barrier((own_pattern, msg))[0]
    x_pattern = swap(later_pattern, everyone, 2)
    x_patterns = jnp.concatenate([later_pattern, x_pattern], axis=0)

    down_1, msg = layer_apply(
        1, recs=recs, blocks=[own, core_blocks], src=src_all, **core_rows
    )
    recs = hop(msg, across_z, even_flips, 1)
    y_core = swap(y_blocks, everyone, 1)
    down_1_x = swap(down_1, starts, 2)
    x_late = swap(own_blocks, early, 2)

    other_rows = dict(patterns=y_patterns, row_flips=(0, 1), blocks=[y_blocks, y_core])
    x_rows = dict(patterns=x_patterns, row_flips=(0, 2))
    down_2, msg = layer_apply(2, recs=recs, src=src_other, **other_rows)
    recs = hop(msg, late, even_flips, 1, own=True)
    down_3, msg = layer_apply(3, recs=recs, blocks=[own, x_blocks], src=src_all, **x_rows)
    recs = hop(msg, everyone, core_flips, 2, own=True)
    up_2, msg = layer_apply(4, recs=recs, states=[down_2], **other_rows)
    recs = chip_hop(msg, across_z, 1, 2)
    up_2_own = swap(up_2[:nb], late_y, 0)
    up_1, msg = layer_apply(
        5, recs=recs, blocks=[own, x_late], states=[down_1, down_1_x], **x_rows
    )
    recs = hop(msg, across_y, core_flips, 2)
    (upper,) = layer_apply(
        6,
        patterns=core_patterns,
        row_flips=(0,),
        recs=recs,
        blocks=[own],
        states=[down_0, up_1, up_2_own, down_3],
    )
    return upper[None]


def solution(mesh):
    return jax.shard_map(
        per_device,
        mesh=mesh,
        in_specs=(
            P("sweep", None, "tile"),
            P("sweep", "tile", None, None, None),
            P("sweep", "tile", None),
        ),
        out_specs=P("sweep", None, "tile"),
        check_vma=False,
    )
```
